32 devices in a mesh: groups: 2 (over y), ctx: 4 (over z), chan: 4 (over x, core).
Axes of the slice: x: 2, y: 2, z: 4, core: 2. Of those that a mesh axis runs over, the one named last changes fastest.
Arguments:
- projections: bfloat16 [3, 256, 16384], P(None, ('groups', 'chan'), 'ctx'), parts along dimension 1, may hold values from -6 to 6
- short_weights: float32 [3, 3, 256], P(None, None, ('groups', 'chan')), parts along dimension 2, may hold values from -3.5 to 3.5
- residues: float32 [256, 16], P(('groups', 'chan')), parts along dimension 0, may hold values from -4 to 4
- rates: float32 [256, 16], P(('groups', 'chan')), parts along dimension 0, may hold values from 0.25 to 512
- skip: float32 [256], P(('groups', 'chan')), parts along dimension 0, may hold values from -3 to 3
Outputs:
- mixer_out: bfloat16 [256, 16384], P(('groups', 'chan'), 'ctx'), parts along dimension 0
The draws below stay inside these ranges and needn't reach their ends.
There are 2 independent parts, one for each index of `groups`. The reference program is written for one: setup_inputs(seed, part) draws one part's arguments, and reference() takes and returns one part's arrays. A program takes and returns all parts, laid end to end along the dimension named above; each array names one. Nothing has to cross between parts.
All inputs are finite; a program needn't handle non-finite values.
Results may differ from the reference program's by a relative error of at most 0.0065.
Values may be sent and summed in bfloat16 or wider, within the bound.
A program may use at most 64 MiB of HBM per device.

```python
import math
import jax
import jax.numpy as jnp
from jax import lax

MODES = 16
TAPS = 3
C = 128
SEQ = 16384


def level_of(key, shape, cuts, smallest, high):
    factor_of, own = 1.0, jax.random.fold_in(key, 6)
    for position, shards_of in cuts:
        steps = jnp.exp(jax.random.uniform(jax.random.fold_in(own, position), (shards_of,), jnp.float32, smallest / len(cuts), high / len(cuts)))
        factor_of = factor_of * jnp.repeat(steps, shape[position] // shards_of).reshape([-1 if axis == position else 1 for axis in range(len(shape))])
    return factor_of


def gaussian(rng, extent, scale, reach, split=(), kind=jnp.bfloat16):
    values = scale * jax.random.normal(rng, extent, jnp.float32)
    if split:
        values = values * level_of(rng, extent, split, -0.22, 0.18)
    return jnp.clip(values, -reach, reach).astype(kind)


def setup_inputs(seed: int = 0, part: int = 0) -> dict:
    splits = jax.random.split(jax.random.key(seed), 6)
    own_keys = jax.random.split(jax.random.fold_in(splits[5], part), 6)
    return {
        "projections": gaussian(own_keys[0], (3, C, SEQ), 1.0, 6.0, ((1, 4), (2, 4))),
        "short_weights": gaussian(own_keys[1], (3, TAPS, C), TAPS ** -0.5, 3.5, ((2, 4),), jnp.float32),
        "residues": gaussian(own_keys[2], (C, MODES), 1.0, 4.0, ((0, 4),), jnp.float32),
        "rates": jnp.clip(jnp.exp(math.log(512.0) - 7.624619 * jax.random.uniform(own_keys[3], (C, MODES), jnp.float32) ** level_of(own_keys[3], (C, MODES), ((0, 4),), -0.2, 0.2)), 0.25, 512.0),
        "skip": gaussian(own_keys[4], (C,), 1.0, 3.0, ((0, 4),), jnp.float32),
    }


def short_filter(stream, tap_weights):
    values = stream.astype(jnp.float32)
    padded = jnp.pad(values, ((0, 0), (TAPS - 1, 0)))
    result = jnp.zeros(values.shape, jnp.float32)
    for offset in range(TAPS):
        start = TAPS - 1 - offset
        result = result + tap_weights[offset][:, None] * padded[:, start:start + SEQ]
    return result.astype(jnp.bfloat16)

def reference(projections, short_weights, residues, rates, skip):
    q_short = short_filter(projections[0], short_weights[0])
    k_short = short_filter(projections[1], short_weights[1])
    v_short = short_filter(projections[2], short_weights[2])
    mixed_in = k_short.astype(jnp.float32) * v_short.astype(jnp.float32)
    decay_rate = rates / SEQ
    mode_coef = residues * jnp.sqrt(2.0 * decay_rate / MODES)
    positions = jnp.arange(SEQ, dtype=jnp.float32)

    def one_filter(pair):
        return lax.optimization_barrier(jnp.sum(pair[0][:, None] * jnp.exp(-(pair[1][:, None] * positions[None, :])), axis=0))
    filters = lax.map(one_filter, (mode_coef, decay_rate))
    length = 2 * SEQ
    spectrum = jnp.fft.rfft(mixed_in, n=length) * jnp.fft.rfft(filters, n=length)
    long_conv = jnp.fft.irfft(spectrum, n=length)[:, :SEQ]
    result = q_short.astype(jnp.float32) * (long_conv + skip[:, None] * mixed_in)
    return result.astype(jnp.bfloat16)
```

```python
import functools

import jax
import jax.numpy as jnp
from jax import lax
from jax.experimental import pallas as pl
from jax.experimental.pallas import tpu as pltpu
from jax.sharding import PartitionSpec as P

LANES = 128


def column(row):
    size = row.shape[1]
    r = lax.broadcasted_iota(jnp.int32, (size, size), 0)
    c = lax.broadcasted_iota(jnp.int32, (size, size), 1)
    spread = jnp.where(r == c, jnp.broadcast_to(row, (size, size)), 0.0)
    return jnp.sum(spread, axis=1, keepdims=True)


def short_block(cur, prev, taps, lane):
    one = jnp.where(lane < 1, pltpu.roll(prev, 1, 1), pltpu.roll(cur, 1, 1))
    two = jnp.where(lane < 2, pltpu.roll(prev, 2, 1), pltpu.roll(cur, 2, 1))
    total = taps[0] * cur + taps[1] * one + taps[2] * two
    return total.astype(jnp.bfloat16).astype(jnp.float32)


def kernel(n, unroll, p_hbm, sw_ref, res_ref, rate_ref, skip_ref, o_hbm,
           pbuf, rim, u, y, e_tab, g_tab, f_tab, s_tab, snd, rcv, obuf,
           in_sems, rim_send, rim_recv, st_send, st_recv, out_sems):
    me = lax.axis_index("ctx")
    _, ch, length = pbuf.shape
    modes = res_ref.shape[1]
    blocks = length // LANES
    seq = n * length

    copies = [
        pltpu.make_async_copy(p_hbm.at[i], pbuf.at[i], in_sems.at[i]) for i in range(3)
    ]
    for i in (1, 2, 0):
        copies[i].start()

    if n > 1:
        barrier = pltpu.get_barrier_semaphore()
        for k in range(1, n):
            pl.semaphore_signal(
                barrier, inc=1, device_id={"ctx": lax.rem(me + k, n)},
                device_id_type=pl.DeviceIdType.MESH,
            )
        pl.semaphore_wait(barrier, n - 1)

    rim_copy = pltpu.make_async_remote_copy(
        src_ref=p_hbm.at[:, :, pl.ds(length - LANES, LANES)],
        dst_ref=rim,
        send_sem=rim_send,
        recv_sem=rim_recv,
        device_id={"ctx": lax.rem(me + 1, n)},
        device_id_type=pl.DeviceIdType.MESH,
    )

    @pl.when(me + 1 < n)
    def _():
        rim_copy.start()

    lane = lax.broadcasted_iota(jnp.int32, (ch, LANES), 1)
    pos = lane.astype(jnp.float32)
    rate = rate_ref[...] / seq
    coef = res_ref[...] * jnp.sqrt(2.0 * rate / modes)
    step_decay = jnp.exp(-(rate * LANES))

    filt = jnp.zeros((ch, LANES), jnp.float32)
    for m in range(modes):
        d = rate[:, m : m + 1]
        a = coef[:, m : m + 1]
        e_tab[pl.ds(m * ch, ch), :] = jnp.exp(-(d * (LANES - 1.0 - pos)))
        filt = filt + a * jnp.exp(-(d * pos))
        g_tab[pl.ds(m * ch, ch), :] = a * jnp.exp(-(d * (pos + 1.0)))
    f_tab[...] = filt

    taps = [
        [jnp.broadcast_to(column(sw_ref[i, j : j + 1, :]), (ch, LANES)) for j in range(3)]
        for i in range(3)
    ]
    skip_col = jnp.broadcast_to(column(skip_ref[...]), (ch, LANES))

    def tile(i, b):
        at = pl.multiple_of(b * LANES, LANES)
        return pbuf[i, :, pl.ds(at, LANES)].astype(jnp.float32)

    copies[1].wait()
    copies[2].wait()

    def mix(b, prev):
        k, v = tile(1, b), tile(2, b)
        ks = short_block(k, prev[0], taps[1], lane)
        vs = short_block(v, prev[1], taps[2], lane)
        u[pl.ds(pl.multiple_of(b * ch, ch), ch), :] = ks * vs
        return k, v

    lax.fori_loop(1, blocks, mix, (tile(1, 0), tile(2, 0)), unroll=False)

    @pl.when(me > 0)
    def _():
        rim_copy.wait_recv()

    @pl.when(me == 0)
    def _():
        rim[...] = jnp.zeros(rim.shape, rim.dtype)

    mix(0, (rim[1].astype(jnp.float32), rim[2].astype(jnp.float32)))

    def states(i, carry):
        for j in range(unroll):
            c = i * unroll + j
            uc = u[pl.ds(c, blocks, stride=ch), :].astype(jnp.bfloat16)
            ec = e_tab[pl.ds(c, modes, stride=ch), :].astype(jnp.bfloat16)
            s_tab[pl.ds(c, blocks, stride=ch), pl.ds(0, modes)] = lax.dot_general(
                uc, ec, (((1,), (1,)), ((), ())), preferred_element_type=jnp.float32
            )
        return carry

    lax.fori_loop(0, ch // unroll, states, 0)

    def local(b, h):
        return h * step_decay + s_tab[pl.ds(pl.multiple_of(b * ch, ch), ch), pl.ds(0, modes)]

    snd[...] = lax.fori_loop(0, blocks, local, jnp.zeros((ch, modes), jnp.float32), unroll=8)

    sends = [
        pltpu.make_async_remote_copy(
            src_ref=snd,
            dst_ref=rcv.at[k - 1],
            send_sem=st_send.at[k - 1],
            recv_sem=st_recv.at[k - 1],
            device_id={"ctx": lax.rem(me + k, n)},
            device_id_type=pl.DeviceIdType.MESH,
        )
        for k in range(1, n)
    ]
    for k in range(1, n):
        @pl.when(me + k < n)
        def _():
            sends[k - 1].start()

    row = lax.broadcasted_iota(jnp.int32, (LANES, LANES), 0)
    col = lax.broadcasted_iota(jnp.int32, (LANES, LANES), 1)
    causal = col >= row

    def intra(i, carry):
        for j in range(unroll):
            c = i * unroll + j
            uc = u[pl.ds(c, blocks, stride=ch), :].astype(jnp.bfloat16)
            spread = jnp.broadcast_to(f_tab[pl.ds(c, 1), :], (LANES, LANES))
            spread = pltpu.roll(spread, 0, 1, stride=1, stride_axis=0)
            toep = jnp.where(causal, spread, 0.0).astype(jnp.bfloat16)
            y[pl.ds(c, blocks, stride=ch), :] = jnp.dot(
                uc, toep, preferred_element_type=jnp.float32
            )
        return carry

    lax.fori_loop(0, ch // unroll, intra, 0)

    for k in range(1, n):
        @pl.when(me >= k)
        def _():
            sends[k - 1].wait_recv()

        @pl.when(me < k)
        def _():
            rcv[k - 1] = jnp.zeros((ch, modes), jnp.float32)

    h0 = jnp.zeros((ch, modes), jnp.float32)
    for k in range(1, n):
        h0 = h0 + rcv[k - 1] * jnp.exp(-(rate * float(length * (k - 1))))

    def scan(b, h):
        at = pl.ds(pl.multiple_of(b * ch, ch), ch)
        s = s_tab[at, pl.ds(0, modes)]
        s_tab[at, pl.ds(0, modes)] = h
        return h * step_decay + s

    lax.fori_loop(0, blocks, scan, h0, unroll=8)

    def inter(i, carry):
        for j in range(unroll):
            c = i * unroll + j
            hc = s_tab[pl.ds(c, blocks, stride=ch), pl.ds(0, modes)].astype(jnp.bfloat16)
            gc = g_tab[pl.ds(c, modes, stride=ch), :].astype(jnp.bfloat16)
            y[pl.ds(c, blocks, stride=ch), :] += jnp.dot(
                hc, gc, preferred_element_type=jnp.float32
            )
        return carry

    lax.fori_loop(0, ch // unroll, inter, 0)

    copies[0].wait()

    def gate(b, prev):
        q = tile(0, b)
        qs = short_block(q, prev, taps[0], lane)
        at = pl.ds(pl.multiple_of(b * ch, ch), ch)
        value = qs * (y[at, :] + skip_col * u[at, :])
        obuf[:, pl.ds(pl.multiple_of(b * LANES, LANES), LANES)] = value.astype(obuf.dtype)
        return q

    pieces = out_sems.shape[0]
    per = blocks // pieces
    prev = rim[0].astype(jnp.float32)
    outs = []
    for piece in range(pieces):
        prev = lax.fori_loop(piece * per, (piece + 1) * per, gate, prev, unroll=False)
        span = pl.ds(piece * per * LANES, per * LANES)
        outs.append(
            pltpu.make_async_copy(obuf.at[:, span], o_hbm.at[:, span], out_sems.at[piece])
        )
        outs[-1].start()

    @pl.when(me + 1 < n)
    def _():
        rim_copy.wait_send()

    for k in range(1, n):
        @pl.when(me + k < n)
        def _():
            sends[k - 1].wait_send()

    for out in outs:
        out.wait()


def shards(projections, short_weights, residues, rates, skip):
    n = lax.axis_size("ctx")
    _, ch, length = projections.shape
    modes = residues.shape[1]
    blocks = length // LANES
    vmem = pl.BlockSpec(memory_space=pltpu.VMEM)
    hbm = pl.BlockSpec(memory_space=pl.ANY)
    return pl.pallas_call(
        functools.partial(kernel, n, 8),
        out_shape=jax.ShapeDtypeStruct((ch, length), jnp.bfloat16),
        in_specs=[hbm, vmem, vmem, vmem, vmem],
        out_specs=hbm,
        scratch_shapes=[
            pltpu.VMEM((3, ch, length), jnp.bfloat16),
            pltpu.VMEM((3, ch, LANES), jnp.bfloat16),
            pltpu.VMEM((blocks * ch, LANES), jnp.float32),
            pltpu.VMEM((blocks * ch, LANES), jnp.float32),
            pltpu.VMEM((modes * ch, LANES), jnp.float32),
            pltpu.VMEM((modes * ch, LANES), jnp.float32),
            pltpu.VMEM((ch, LANES), jnp.float32),
            pltpu.VMEM((blocks * ch, LANES), jnp.float32),
            pltpu.VMEM((ch, modes), jnp.float32),
            pltpu.VMEM((n - 1, ch, modes), jnp.float32),
            pltpu.VMEM((ch, length), jnp.bfloat16),
            pltpu.SemaphoreType.DMA((3,)),
            pltpu.SemaphoreType.DMA,
            pltpu.SemaphoreType.DMA,
            pltpu.SemaphoreType.DMA((n - 1,)),
            pltpu.SemaphoreType.DMA((n - 1,)),
            pltpu.SemaphoreType.DMA((4,)),
        ],
        compiler_params=pltpu.CompilerParams(
            collective_id=0, has_side_effects=True, vmem_limit_bytes=32 * 1024 * 1024
        ),
        name="mixer",
    )(projections, short_weights, residues, rates, skip[None, :])


def solution(mesh):
    return jax.shard_map(
        shards,
        mesh=mesh,
        in_specs=(
            P(None, ("groups", "chan"), "ctx"),
            P(None, None, ("groups", "chan")),
            P(("groups", "chan"), None),
            P(("groups", "chan"), None),
            P(("groups", "chan")),
        ),
        out_specs=P(("groups", "chan"), "ctx"),
        check_vma=False,
    )
```

```python
import functools

import jax
import jax.numpy as jnp
from jax import lax
from jax.experimental import pallas as pl
from jax.experimental.pallas import tpu as pltpu
from jax.sharding import PartitionSpec as P

LANES = 128


def column(row):
    size = row.shape[1]
    r = lax.broadcasted_iota(jnp.int32, (size, size), 0)
    c = lax.broadcasted_iota(jnp.int32, (size, size), 1)
    spread = jnp.where(r == c, jnp.broadcast_to(row, (size, size)), 0.0)
    return jnp.sum(spread, axis=1, keepdims=True)


def short_block(cur, prev, taps, lane):
    one = jnp.where(lane < 1, pltpu.roll(prev, 1, 1), pltpu.roll(cur, 1, 1))
    two = jnp.where(lane < 2, pltpu.roll(prev, 2, 1), pltpu.roll(cur, 2, 1))
    total = taps[0] * cur + taps[1] * one + taps[2] * two
    return total.astype(jnp.bfloat16).astype(jnp.float32)


def kernel(n, unroll, p_hbm, sw_hbm, res_hbm, rate_hbm, skip_hbm, o_ref,
           sw_ref, res_ref, rate_ref, skip_ref, pbuf, rim, u, y, e_tab, g_tab, f_tab, s_tab, p_tab, h_in, snd, rcv,
           in_sems, rim_send, rim_recv, st_send, st_recv):
    me = lax.axis_index("ctx")
    _, ch, length = pbuf.shape
    modes = res_ref.shape[0]
    blocks = length // LANES
    seq = n * length

    copies = [
        pltpu.make_async_copy(p_hbm.at[i], pbuf.at[i], in_sems.at[i]) for i in range(3)
    ]
    small = ((rate_hbm, rate_ref), (res_hbm, res_ref), (sw_hbm, sw_ref), (skip_hbm, skip_ref))
    for i, (source, target) in enumerate(small):
        copies.append(pltpu.make_async_copy(source, target, in_sems.at[3 + i]))
    for i in (3, 4, 5, 6, 1, 2, 0):
        copies[i].start()

    if n > 1:
        barrier = pltpu.get_barrier_semaphore()
        for k in range(1, n):
            pl.semaphore_signal(
                barrier, inc=1, device_id={"ctx": lax.rem(me + k, n)},
                device_id_type=pl.DeviceIdType.MESH,
            )

    rim_copy = pltpu.make_async_remote_copy(
        src_ref=p_hbm.at[:, :, pl.ds(length - LANES, LANES)],
        dst_ref=rim,
        send_sem=rim_send,
        recv_sem=rim_recv,
        device_id={"ctx": lax.rem(me + 1, n)},
        device_id_type=pl.DeviceIdType.MESH,
    )

    lane = lax.broadcasted_iota(jnp.int32, (ch, LANES), 1)
    pos = lane.astype(jnp.float32)
    for i in (3, 4, 5, 6):
        copies[i].wait()
    rate = rate_ref[...].T / seq
    coef = res_ref[...].T * jnp.sqrt(2.0 * rate / modes)
    step_decay = jnp.exp(-(rate * LANES))

    filt = jnp.zeros((ch, LANES), jnp.float32)
    for m in range(modes):
        d = rate[:, m : m + 1]
        a = coef[:, m : m + 1]
        e_tab[pl.ds(m * ch, ch), :] = jnp.exp(-(d * (LANES - 1.0 - pos)))
        filt = filt + a * jnp.exp(-(d * pos))
        g_tab[pl.ds(m * ch, ch), :] = a * jnp.exp(-(d * (pos + 1.0)))
    f_tab[...] = filt

    taps = [
        [jnp.broadcast_to(column(sw_ref[i, j : j + 1, :]), (ch, LANES)) for j in range(3)]
        for i in range(3)
    ]
    skip_col = jnp.broadcast_to(column(skip_ref[...]), (ch, LANES))

    if n > 1:
        pl.semaphore_wait(barrier, n - 1)

    @pl.when(me + 1 < n)
    def _():
        rim_copy.start()

    def tile(i, b):
        at = pl.multiple_of(b * LANES, LANES)
        return pbuf[i, :, pl.ds(at, LANES)].astype(jnp.float32)

    copies[1].wait()
    copies[2].wait()

    def mix(b, prev):
        k, v = tile(1, b), tile(2, b)
        ks = short_block(k, prev[0], taps[1], lane)
        vs = short_block(v, prev[1], taps[2], lane)
        u[pl.ds(pl.multiple_of(b * ch, ch), ch), :] = ks * vs
        return k, v

    zero = jnp.zeros((ch, LANES), jnp.float32)
    lax.fori_loop(0, blocks, mix, (zero, zero), unroll=8)
    u[pl.ds(0, ch), :] = jnp.where(lane < 2, 0.0, u[pl.ds(0, ch), :])

    def states(i, carry):
        for j in range(unroll):
            c = i * unroll + j
            uc = u[pl.ds(c, blocks, stride=ch), :].astype(jnp.bfloat16)
            ec = e_tab[pl.ds(c, modes, stride=ch), :].astype(jnp.bfloat16)
            s_tab[pl.ds(c, blocks, stride=ch), pl.ds(0, modes)] = lax.dot_general(
                uc, ec, (((1,), (1,)), ((), ())), preferred_element_type=jnp.float32
            )
        return carry

    lax.fori_loop(0, ch // unroll, states, 0)

    def local(b, state):
        h, p = state
        at = pl.ds(pl.multiple_of(b * ch, ch), ch)
        s = s_tab[at, pl.ds(0, modes)]
        s_tab[at, pl.ds(0, modes)] = h
        p_tab[at, pl.ds(0, modes)] = p
        return h * step_decay + s, p * step_decay

    first = (jnp.zeros((ch, modes), jnp.float32), jnp.ones((ch, modes), jnp.float32))
    end, whole = lax.fori_loop(0, blocks, local, first, unroll=8)

    @pl.when(me > 0)
    def _():
        rim_copy.wait_recv()

    @pl.when(me == 0)
    def _():
        rim[...] = jnp.zeros(rim.shape, rim.dtype)

    mix(0, (rim[1].astype(jnp.float32), rim[2].astype(jnp.float32)))
    edge = u[pl.ds(0, ch), :]
    early = jnp.exp(-(rate * (LANES - 1.0))) * edge[:, 0:1] + jnp.exp(
        -(rate * (LANES - 2.0))
    ) * edge[:, 1:2]
    snd[...] = end + jnp.exp(-(rate * float(length - LANES))) * early

    sends = [
        pltpu.make_async_remote_copy(
            src_ref=snd,
            dst_ref=rcv.at[k - 1],
            send_sem=st_send.at[k - 1],
            recv_sem=st_recv.at[k - 1],
            device_id={"ctx": lax.rem(me + k, n)},
            device_id_type=pl.DeviceIdType.MESH,
        )
        for k in range(1, n)
    ]
    for k in range(1, n):
        @pl.when(me + k < n)
        def _():
            sends[k - 1].start()

    def add_early(b, p):
        at = pl.ds(pl.multiple_of(b * ch, ch), ch)
        s_tab[at, pl.ds(0, modes)] = s_tab[at, pl.ds(0, modes)] + p * early
        return p_tab[at, pl.ds(0, modes)]

    lax.fori_loop(0, blocks, add_early, jnp.zeros((ch, modes), jnp.float32), unroll=8)

    row = lax.broadcasted_iota(jnp.int32, (LANES, LANES), 0)
    col = lax.broadcasted_iota(jnp.int32, (LANES, LANES), 1)
    causal = col >= row

    def intra(i, carry):
        for j in range(unroll):
            c = i * unroll + j
            uc = u[pl.ds(c, blocks, stride=ch), :].astype(jnp.bfloat16)
            spread = jnp.broadcast_to(f_tab[pl.ds(c, 1), :], (LANES, LANES))
            spread = pltpu.roll(spread, 0, 1, stride=1, stride_axis=0)
            toep = jnp.where(causal, spread, 0.0).astype(jnp.bfloat16)
            y[pl.ds(c, blocks, stride=ch), :] = jnp.dot(
                uc, toep, preferred_element_type=jnp.float32
            )
        return carry

    lax.fori_loop(0, ch // unroll, intra, 0)

    copies[0].wait()

    def ahead(b, prev):
        q = tile(0, b)
        at = pl.ds(pl.multiple_of(b * ch, ch), ch)
        y[at, :] = y[at, :] + skip_col * u[at, :]
        u[at, :] = short_block(q, prev, taps[0], lane)
        return q

    lax.fori_loop(0, blocks, ahead, rim[0].astype(jnp.float32), unroll=8)

    for k in range(1, n):
        @pl.when(me >= k)
        def _():
            sends[k - 1].wait_recv()

        @pl.when(me < k)
        def _():
            rcv[k - 1] = jnp.zeros((ch, modes), jnp.float32)

    h0 = jnp.zeros((ch, modes), jnp.float32)
    for k in range(1, n):
        h0 = h0 + rcv[k - 1] * jnp.exp(-(rate * float(length * (k - 1))))
    h_in[...] = h0

    def inter(i, carry):
        for j in range(unroll):
            c = i * unroll + j
            hc = s_tab[pl.ds(c, blocks, stride=ch), pl.ds(0, modes)]
            pc = p_tab[pl.ds(c, blocks, stride=ch), pl.ds(0, modes)]
            hc = (hc + pc * h_in[pl.ds(c, 1), :]).astype(jnp.bfloat16)
            gc = g_tab[pl.ds(c, modes, stride=ch), :].astype(jnp.bfloat16)
            y[pl.ds(c, blocks, stride=ch), :] += jnp.dot(
                hc, gc, preferred_element_type=jnp.float32
            )
        return carry

    lax.fori_loop(0, ch // unroll, inter, 0)

    def gate(b, carry):
        at = pl.ds(pl.multiple_of(b * ch, ch), ch)
        value = u[at, :] * y[at, :]
        o_ref[:, pl.ds(pl.multiple_of(b * LANES, LANES), LANES)] = value.astype(o_ref.dtype)
        return carry

    lax.fori_loop(0, blocks, gate, 0, unroll=8)

    @pl.when(me + 1 < n)
    def _():
        rim_copy.wait_send()

    for k in range(1, n):
        @pl.when(me + k < n)
        def _():
            sends[k - 1].wait_send()


def shards(projections, short_weights, residues, rates, skip):
    n = lax.axis_size("ctx")
    _, ch, length = projections.shape
    modes = residues.shape[1]
    blocks = length // LANES
    vmem = pl.BlockSpec(memory_space=pltpu.VMEM)
    hbm = pl.BlockSpec(memory_space=pltpu.HBM)
    return pl.pallas_call(
        functools.partial(kernel, n, 8),
        out_shape=jax.ShapeDtypeStruct((ch, length), jnp.bfloat16),
        in_specs=[hbm] * 5,
        out_specs=vmem,
        scratch_shapes=[
            pltpu.VMEM(short_weights.shape, jnp.float32),
            pltpu.VMEM((modes, ch), jnp.float32),
            pltpu.VMEM((modes, ch), jnp.float32),
            pltpu.VMEM((1, ch), jnp.float32),
            pltpu.VMEM((3, ch, length), jnp.bfloat16),
            pltpu.VMEM((3, ch, LANES), jnp.bfloat16),
            pltpu.VMEM((blocks * ch, LANES), jnp.float32),
            pltpu.VMEM((blocks * ch, LANES), jnp.float32),
            pltpu.VMEM((modes * ch, LANES), jnp.float32),
            pltpu.VMEM((modes * ch, LANES), jnp.float32),
            pltpu.VMEM((ch, LANES), jnp.float32),
            pltpu.VMEM((blocks * ch, LANES), jnp.float32),
            pltpu.VMEM((blocks * ch, LANES), jnp.float32),
            pltpu.VMEM((ch, modes), jnp.float32),
            pltpu.VMEM((ch, modes), jnp.float32),
            pltpu.VMEM((n - 1, ch, modes), jnp.float32),
            pltpu.SemaphoreType.DMA((7,)),
            pltpu.SemaphoreType.DMA,
            pltpu.SemaphoreType.DMA,
            pltpu.SemaphoreType.DMA((n - 1,)),
            pltpu.SemaphoreType.DMA((n - 1,)),
        ],
        compiler_params=pltpu.CompilerParams(
            collective_id=0, has_side_effects=True, vmem_limit_bytes=32 * 1024 * 1024
        ),
        name="mixer",
    )(*(
        pltpu.with_memory_space_constraint(a, pltpu.HBM)
        for a in (projections, short_weights, residues.T, rates.T, skip[None, :])
    ))


def solution(mesh):
    return jax.shard_map(
        shards,
        mesh=mesh,
        in_specs=(
            P(None, ("groups", "chan"), "ctx"),
            P(None, None, ("groups", "chan")),
            P(("groups", "chan"), None),
            P(("groups", "chan"), None),
            P(("groups", "chan")),
        ),
        out_specs=P(("groups", "chan"), "ctx"),
        check_vma=False,
    )
```

```python
import functools

import jax
import jax.numpy as jnp
from jax import lax
from jax.experimental import pallas as pl
from jax.experimental.pallas import tpu as pltpu
from jax.sharding import PartitionSpec as P

LANES = 128
PAD = 8
K_HEAD, V_HEAD, K_TAIL, V_TAIL, Q_TAIL = 18, 22, 24, 28, 32


def column(row):
    size = row.shape[1]
    r = lax.broadcasted_iota(jnp.int32, (size, size), 0)
    c = lax.broadcasted_iota(jnp.int32, (size, size), 1)
    spread = jnp.where(r == c, jnp.broadcast_to(row, (size, size)), 0.0)
    return jnp.sum(spread, axis=1, keepdims=True)


def short_block(cur, prev, taps, lane):
    one = jnp.where(lane < 1, pltpu.roll(prev, 1, 1), pltpu.roll(cur, 1, 1))
    two = jnp.where(lane < 2, pltpu.roll(prev, 2, 1), pltpu.roll(cur, 2, 1))
    total = taps[0] * cur + taps[1] * one + taps[2] * two
    return total.astype(jnp.bfloat16).astype(jnp.float32)


def kernel(n, unroll, p_hbm, sw_hbm, res_hbm, rate_hbm, skip_hbm, o_ref,
           sw_ref, res_ref, rate_ref, skip_ref, pbuf, u, y, e_tab, g_tab, f_tab, s_tab, h_tab, p_tab, h_in, q_tab, v_tab, z, snd, rcv,
           in_sems, st_send, st_recv):
    me = lax.axis_index("ctx")
    _, ch, length = pbuf.shape
    modes = res_ref.shape[0]
    blocks = length // LANES
    seq = n * length
    pit = ch + PAD

    copies = [
        pltpu.make_async_copy(p_hbm.at[i], pbuf.at[i], in_sems.at[i]) for i in range(3)
    ]
    small = ((rate_hbm, rate_ref), (res_hbm, res_ref), (sw_hbm, sw_ref), (skip_hbm, skip_ref))
    for i, (source, target) in enumerate(small):
        copies.append(pltpu.make_async_copy(source, target, in_sems.at[3 + i]))
    for i in (3, 4, 5, 6, 1, 2, 0):
        copies[i].start()

    barrier = pltpu.get_barrier_semaphore()
    for k in range(1, n):
        pl.semaphore_signal(
            barrier, inc=1, device_id={"ctx": lax.rem(me + k, n)},
            device_id_type=pl.DeviceIdType.MESH,
        )

    lane = lax.broadcasted_iota(jnp.int32, (ch, LANES), 1)
    pos = lane.astype(jnp.float32)
    for i in (3, 4, 5, 6):
        copies[i].wait()
    rate = rate_ref[...].T / seq
    coef = res_ref[...].T * jnp.sqrt(2.0 * rate / modes)
    step_decay = jnp.exp(-(rate * LANES))

    filt = jnp.zeros((ch, LANES), jnp.float32)
    for m in range(modes):
        d = rate[:, m : m + 1]
        a = coef[:, m : m + 1]
        e_tab[pl.ds(m * pit, ch), :] = jnp.exp(-(d * (LANES - 1.0 - pos)))
        filt = filt + a * jnp.exp(-(d * pos))
        g_tab[pl.ds(m * pit, ch), :] = a * jnp.exp(-(d * (pos + 1.0)))
    f_tab[...] = filt

    taps = [
        [jnp.broadcast_to(column(sw_ref[i, j : j + 1, :]), (ch, LANES)) for j in range(3)]
        for i in range(3)
    ]
    skip_col = jnp.broadcast_to(column(skip_ref[...]), (ch, LANES))

    def tile(i, b):
        at = pl.multiple_of(b * LANES, LANES)
        return pbuf[i, :, pl.ds(at, LANES)].astype(jnp.float32)

    copies[1].wait()
    copies[2].wait()

    def mix(b, prev):
        k, v = tile(1, b), tile(2, b)
        ks = short_block(k, prev[0], taps[1], lane)
        vs = short_block(v, prev[1], taps[2], lane)
        u[pl.ds(pl.multiple_of(b * pit, 8), ch), :] = ks * vs
        return k, v

    zero = jnp.zeros((ch, LANES), jnp.float32)
    lax.fori_loop(0, blocks, mix, (zero, zero), unroll=8)
    u[pl.ds(0, ch), :] = jnp.where(lane < 2, 0.0, u[pl.ds(0, ch), :])

    def states(i, carry):
        for j in range(unroll):
            c = i * unroll + j
            uc = u[pl.ds(c, blocks, stride=pit), :].astype(jnp.bfloat16)
            ec = e_tab[pl.ds(c, modes, stride=pit), :].astype(jnp.bfloat16)
            s_tab[pl.ds(c, blocks, stride=pit), pl.ds(0, modes)] = lax.dot_general(
                uc, ec, (((1,), (1,)), ((), ())), preferred_element_type=jnp.float32
            )
        return carry

    lax.fori_loop(0, ch // unroll, states, 0)

    def local(b, state):
        h, p = state
        at = pl.ds(pl.multiple_of(b * pit, 8), ch)
        s = s_tab[at, pl.ds(0, modes)]
        h_tab[at, pl.ds(0, modes)] = h
        p_tab[at, pl.ds(0, modes)] = p
        return h * step_decay + s, p * step_decay

    first = (jnp.zeros((ch, modes), jnp.float32), jnp.ones((ch, modes), jnp.float32))
    end, whole = lax.fori_loop(0, blocks, local, first, unroll=8)

    def pair(value, source, target):
        here = (lane >= target) & (lane < target + 2)
        return jnp.where(here, pltpu.roll(value, (target - source) % LANES, 1), 0.0)

    copies[0].wait()
    last = blocks - 1
    snd[...] = (
        pair(tile(1, 0), 0, K_HEAD)
        + pair(tile(2, 0), 0, V_HEAD)
        + pair(tile(1, last), LANES - 2, K_TAIL)
        + pair(tile(2, last), LANES - 2, V_TAIL)
        + pair(tile(0, last), LANES - 2, Q_TAIL)
    )
    snd[:, pl.ds(0, modes)] = end

    pl.semaphore_wait(barrier, n - 1)
    sends = [
        pltpu.make_async_remote_copy(
            src_ref=snd,
            dst_ref=rcv.at[k - 1],
            send_sem=st_send.at[k - 1],
            recv_sem=st_recv.at[k - 1],
            device_id={"ctx": lax.rem(me + k, n)},
            device_id_type=pl.DeviceIdType.MESH,
        )
        for k in range(1, n)
    ]
    for k in range(1, n):
        @pl.when(me + k < n)
        def _():
            sends[k - 1].start()

    row = lax.broadcasted_iota(jnp.int32, (LANES, LANES), 0)
    col = lax.broadcasted_iota(jnp.int32, (LANES, LANES), 1)
    causal = col >= row

    def intra(i, carry):
        for j in range(unroll):
            c = i * unroll + j
            uc = u[pl.ds(c, blocks, stride=pit), :].astype(jnp.bfloat16)
            spread = jnp.broadcast_to(f_tab[pl.ds(c, 1), :], (LANES, LANES))
            spread = pltpu.roll(spread, 0, 1, stride=1, stride_axis=0)
            toep = jnp.where(causal, spread, 0.0).astype(jnp.bfloat16)
            y[pl.ds(c, blocks, stride=pit), :] = jnp.dot(
                uc, toep, preferred_element_type=jnp.float32
            )
        return carry

    lax.fori_loop(0, ch // unroll, intra, 0)

    def ahead(b, prev):
        q = tile(0, b)
        at = pl.ds(pl.multiple_of(b * pit, 8), ch)
        v_tab[at, :] = y[at, :] + skip_col * u[at, :]
        q_tab[at, :] = short_block(q, prev, taps[0], lane)
        return q

    lax.fori_loop(0, blocks, ahead, zero, unroll=8)

    is_k = (lane >= K_HEAD - 2) & (lane < K_HEAD + 2)
    edge_taps = [jnp.where(is_k, taps[1][j], taps[2][j]) for j in range(3)]
    far = [jnp.exp(-(rate * float(length * k))) for k in range(n - 1)]
    far_first = jnp.exp(-(rate * (length - 1.0)))
    far_second = jnp.exp(-(rate * (length - 2.0)))
    near_first, near_second = jnp.exp(rate), jnp.exp(2.0 * rate)
    filt_next = jnp.where(lane < 1, 0.0, pltpu.roll(filt, 1, 1))

    for k in range(1, n):
        @pl.when(me >= k)
        def _():
            sends[k - 1].wait_recv()

        @pl.when(me < k)
        def _():
            rcv[k - 1] = jnp.zeros((ch, LANES), jnp.float32)

    h0 = jnp.zeros((ch, modes), jnp.float32)
    for k in range(1, n):
        message = rcv[k - 1]
        ends = message
        if k + 1 < n:
            ends = message + pltpu.roll(rcv[k], LANES - (K_TAIL - K_HEAD + 2), 1)
        shorts = (
            edge_taps[0] * ends
            + edge_taps[1] * pltpu.roll(ends, 1, 1)
            + edge_taps[2] * pltpu.roll(ends, 2, 1)
        ).astype(jnp.bfloat16).astype(jnp.float32)
        firsts = shorts * pltpu.roll(shorts, LANES - (V_HEAD - K_HEAD), 1)
        state = (
            message[:, :modes]
            + far_first * firsts[:, K_HEAD : K_HEAD + 1]
            + far_second * firsts[:, K_HEAD + 1 : K_HEAD + 2]
        )
        h0 = h0 + far[k - 1] * state

    before = rcv[0]
    block = pl.ds(0, ch)
    ks = short_block(tile(1, 0), pltpu.roll(before, LANES - 2 - K_TAIL, 1), taps[1], lane)
    vs = short_block(tile(2, 0), pltpu.roll(before, LANES - 2 - V_TAIL, 1), taps[2], lane)
    q_tab[block, :] = short_block(
        tile(0, 0), pltpu.roll(before, LANES - 2 - Q_TAIL, 1), taps[0], lane
    )
    firsts = ks * vs
    one, two = firsts[:, 0:1], firsts[:, 1:2]
    v_tab[block, :] = (
        v_tab[block, :]
        + skip_col * jnp.where(lane < 2, firsts, 0.0)
        + filt * one
        + filt_next * two
    )
    own = near_first * one + near_second * two
    h_in[...] = h0 + own
    h_tab[block, pl.ds(0, modes)] = -own

    def inter(i, carry):
        for j in range(unroll):
            c = i * unroll + j
            hc = h_tab[pl.ds(c, blocks, stride=pit), pl.ds(0, modes)]
            pc = p_tab[pl.ds(c, blocks, stride=pit), pl.ds(0, modes)]
            hc = (hc + pc * h_in[pl.ds(c, 1), :]).astype(jnp.bfloat16)
            gc = g_tab[pl.ds(c, modes, stride=pit), :].astype(jnp.bfloat16)
            z[pl.ds(c, blocks, stride=pit), :] = jnp.dot(
                hc, gc, preferred_element_type=jnp.float32
            )
        return carry

    lax.fori_loop(0, ch // unroll, inter, 0)

    def gate(b, carry):
        at = pl.ds(pl.multiple_of(b * pit, 8), ch)
        value = q_tab[at, :] * (v_tab[at, :] + z[at, :])
        o_ref[:, pl.ds(pl.multiple_of(b * LANES, LANES), LANES)] = value.astype(o_ref.dtype)
        return carry

    lax.fori_loop(0, blocks, gate, 0, unroll=8)

    for k in range(1, n):
        @pl.when(me + k < n)
        def _():
            sends[k - 1].wait_send()


def shards(projections, short_weights, residues, rates, skip):
    n = lax.axis_size("ctx")
    _, ch, length = projections.shape
    modes = residues.shape[1]
    blocks = length // LANES
    pit = ch + PAD
    vmem = pl.BlockSpec(memory_space=pltpu.VMEM)
    hbm = pl.BlockSpec(memory_space=pltpu.HBM)
    return pl.pallas_call(
        functools.partial(kernel, n, 16),
        out_shape=jax.ShapeDtypeStruct((ch, length), jnp.bfloat16),
        in_specs=[hbm] * 5,
        out_specs=vmem,
        scratch_shapes=[
            pltpu.VMEM(short_weights.shape, jnp.float32),
            pltpu.VMEM((modes, ch), jnp.float32),
            pltpu.VMEM((modes, ch), jnp.float32),
            pltpu.VMEM((1, ch), jnp.float32),
            pltpu.VMEM((3, ch, length), jnp.bfloat16),
            pltpu.VMEM((blocks * pit, LANES), jnp.float32),
            pltpu.VMEM((blocks * pit, LANES), jnp.float32),
            pltpu.VMEM((modes * pit, LANES), jnp.float32),
            pltpu.VMEM((modes * pit, LANES), jnp.float32),
            pltpu.VMEM((ch, LANES), jnp.float32),
            pltpu.VMEM((blocks * pit, LANES), jnp.float32),
            pltpu.VMEM((blocks * pit, LANES), jnp.float32),
            pltpu.VMEM((blocks * pit, LANES), jnp.float32),
            pltpu.VMEM((ch, modes), jnp.float32),
            pltpu.VMEM((blocks * pit, LANES), jnp.float32),
            pltpu.VMEM((blocks * pit, LANES), jnp.float32),
            pltpu.VMEM((blocks * pit, LANES), jnp.float32),
            pltpu.VMEM((ch, LANES), jnp.float32),
            pltpu.VMEM((n - 1, ch, LANES), jnp.float32),
            pltpu.SemaphoreType.DMA((7,)),
            pltpu.SemaphoreType.DMA((n - 1,)),
            pltpu.SemaphoreType.DMA((n - 1,)),
        ],
        compiler_params=pltpu.CompilerParams(
            collective_id=0, has_side_effects=True, vmem_limit_bytes=32 * 1024 * 1024
        ),
        name="mixer",
    )(*(
        pltpu.with_memory_space_constraint(a, pltpu.HBM)
        for a in (projections, short_weights, residues.T, rates.T, skip[None, :])
    ))


def solution(mesh):
    return jax.shard_map(
        shards,
        mesh=mesh,
        in_specs=(
            P(None, ("groups", "chan"), "ctx"),
            P(None, None, ("groups", "chan")),
            P(("groups", "chan"), None),
            P(("groups", "chan"), None),
            P(("groups", "chan")),
        ),
        out_specs=P(("groups", "chan"), "ctx"),
        check_vma=False,
    )
```

```python
import functools

import jax
import jax.numpy as jnp
from jax import lax
from jax.experimental import pallas as pl
from jax.experimental.pallas import tpu as pltpu
from jax.sharding import PartitionSpec as P

LANES = 128
PAD = 8
K_HEAD, V_HEAD, K_TAIL, V_TAIL, Q_TAIL = 18, 22, 24, 28, 30
FIELD = 32


def column(row):
    size = row.shape[1]
    r = lax.broadcasted_iota(jnp.int32, (size, size), 0)
    c = lax.broadcasted_iota(jnp.int32, (size, size), 1)
    spread = jnp.where(r == c, jnp.broadcast_to(row, (size, size)), 0.0)
    return jnp.sum(spread, axis=1, keepdims=True)


def short_block(cur, prev, taps, lane):
    one = jnp.where(lane < 1, pltpu.roll(prev, 1, 1), pltpu.roll(cur, 1, 1))
    two = jnp.where(lane < 2, pltpu.roll(prev, 2, 1), pltpu.roll(cur, 2, 1))
    total = taps[0] * cur + taps[1] * one + taps[2] * two
    return total.astype(jnp.bfloat16).astype(jnp.float32)


def kernel(n, unroll, p_hbm, sw_hbm, res_hbm, rate_hbm, skip_hbm, o_ref,
           sw_ref, res_ref, rate_ref, skip_ref, pbuf, u, y, e_tab, g_tab, f_tab, s_tab, h_tab, p_tab, h_in, q_tab, v_tab, z, wide, snd, rcv,
           in_sems, st_send, st_recv):
    me = lax.axis_index("ctx")
    _, ch, length = pbuf.shape
    modes = res_ref.shape[0]
    blocks = length // LANES
    seq = n * length
    pit = ch + PAD

    barrier = pltpu.get_barrier_semaphore()
    for k in range(1, n):
        @pl.when(me >= k)
        def _():
            pl.semaphore_signal(
                barrier, inc=1, device_id={"ctx": lax.rem(me + n - k, n)},
                device_id_type=pl.DeviceIdType.MESH,
            )

    copies = [
        pltpu.make_async_copy(p_hbm.at[i], pbuf.at[i], in_sems.at[i]) for i in range(3)
    ]
    small = ((rate_hbm, rate_ref), (res_hbm, res_ref), (sw_hbm, sw_ref), (skip_hbm, skip_ref))
    for i, (source, target) in enumerate(small):
        copies.append(pltpu.make_async_copy(source, target, in_sems.at[3 + i]))
    for i in (3, 4, 5, 6, 1, 2, 0):
        copies[i].start()

    lane = lax.broadcasted_iota(jnp.int32, (ch, LANES), 1)
    pos = lane.astype(jnp.float32)
    for i in (3, 4, 5, 6):
        copies[i].wait()
    rate = rate_ref[...].T / seq
    coef = res_ref[...].T * jnp.sqrt(2.0 * rate / modes)
    step_decay = jnp.exp(-(rate * LANES))

    filt = jnp.zeros((ch, LANES), jnp.float32)
    for m in range(modes):
        d = rate[:, m : m + 1]
        a = coef[:, m : m + 1]
        e_tab[pl.ds(m * pit, ch), :] = jnp.exp(-(d * (LANES - 1.0 - pos)))
        filt = filt + a * jnp.exp(-(d * pos))
        g_tab[pl.ds(m * pit, ch), :] = a * jnp.exp(-(d * (pos + 1.0)))
    f_tab[...] = filt

    taps = [
        [jnp.broadcast_to(column(sw_ref[i, j : j + 1, :]), (ch, LANES)) for j in range(3)]
        for i in range(3)
    ]
    skip_col = jnp.broadcast_to(column(skip_ref[...]), (ch, LANES))

    def tile(i, b):
        at = pl.multiple_of(b * LANES, LANES)
        return pbuf[i, :, pl.ds(at, LANES)].astype(jnp.float32)

    copies[1].wait()
    copies[2].wait()

    def mix(b, prev):
        k, v = tile(1, b), tile(2, b)
        ks = short_block(k, prev[0], taps[1], lane)
        vs = short_block(v, prev[1], taps[2], lane)
        u[pl.ds(pl.multiple_of(b * pit, 8), ch), :] = ks * vs
        return k, v

    zero = jnp.zeros((ch, LANES), jnp.float32)
    lax.fori_loop(0, blocks, mix, (zero, zero), unroll=8)
    u[pl.ds(0, ch), :] = jnp.where(lane < 2, 0.0, u[pl.ds(0, ch), :])

    def states(i, carry):
        for j in range(unroll):
            c = i * unroll + j
            uc = u[pl.ds(c, blocks, stride=pit), :].astype(jnp.bfloat16)
            ec = e_tab[pl.ds(c, modes, stride=pit), :].astype(jnp.bfloat16)
            s_tab[pl.ds(c, blocks, stride=pit), pl.ds(0, modes)] = lax.dot_general(
                uc, ec, (((1,), (1,)), ((), ())), preferred_element_type=jnp.float32
            )
        return carry

    lax.fori_loop(0, ch // unroll, states, 0)

    def local(b, state):
        h, p = state
        at = pl.ds(pl.multiple_of(b * pit, 8), ch)
        s = s_tab[at, pl.ds(0, modes)]
        h_tab[at, pl.ds(0, modes)] = h
        p_tab[at, pl.ds(0, modes)] = p
        return h * step_decay + s, p * step_decay

    first = (jnp.zeros((ch, modes), jnp.float32), jnp.ones((ch, modes), jnp.float32))
    end, whole = lax.fori_loop(0, blocks, local, first, unroll=8)

    def pair(value, source, target):
        here = (lane >= target) & (lane < target + 2)
        return jnp.where(here, pltpu.roll(value, (target - source) % LANES, 1), 0.0)

    copies[0].wait()
    last = blocks - 1
    edges = (
        pair(tile(1, 0), 0, K_HEAD)
        + pair(tile(2, 0), 0, V_HEAD)
        + pair(tile(1, last), LANES - 2, K_TAIL)
        + pair(tile(2, last), LANES - 2, V_TAIL)
        + pair(tile(0, last), LANES - 2, Q_TAIL)
    )
    wide[...] = edges
    wide[:, pl.ds(0, modes)] = end
    rows = ch * FIELD // LANES
    snd[...] = sum(
        pltpu.roll(wide[pl.ds(g * rows, rows), :], g * FIELD, 1) if g else wide[pl.ds(0, rows), :]
        for g in range(ch // rows)
    )

    sends = [
        pltpu.make_async_remote_copy(
            src_ref=snd,
            dst_ref=rcv.at[k - 1],
            send_sem=st_send.at[k - 1],
            recv_sem=st_recv.at[k - 1],
            device_id={"ctx": lax.rem(me + k, n)},
            device_id_type=pl.DeviceIdType.MESH,
        )
        for k in range(1, n)
    ]

    def send():
        pl.semaphore_wait(barrier, n - 1 - me)
        for k in range(1, n):
            @pl.when(me + k < n)
            def _():
                sends[k - 1].start()

    @pl.when((me > 0) & (me < n - 1))
    def _():
        send()

    row = lax.broadcasted_iota(jnp.int32, (LANES, LANES), 0)
    col = lax.broadcasted_iota(jnp.int32, (LANES, LANES), 1)
    causal = col >= row

    def intra(i, carry):
        for j in range(unroll):
            c = i * unroll + j
            uc = u[pl.ds(c, blocks, stride=pit), :].astype(jnp.bfloat16)
            spread = jnp.broadcast_to(f_tab[pl.ds(c, 1), :], (LANES, LANES))
            spread = pltpu.roll(spread, 0, 1, stride=1, stride_axis=0)
            toep = jnp.where(causal, spread, 0.0).astype(jnp.bfloat16)
            y[pl.ds(c, blocks, stride=pit), :] = jnp.dot(
                uc, toep, preferred_element_type=jnp.float32
            )
        return carry

    lax.fori_loop(0, ch // unroll, intra, 0)

    @pl.when(me == 0)
    def _():
        send()

    def ahead(b, prev):
        q = tile(0, b)
        at = pl.ds(pl.multiple_of(b * pit, 8), ch)
        v_tab[at, :] = y[at, :] + skip_col * u[at, :]
        q_tab[at, :] = short_block(q, prev, taps[0], lane)
        return q

    lax.fori_loop(0, blocks, ahead, zero, unroll=8)

    is_tail = ((lane >= K_HEAD - 2) & (lane < K_HEAD)) | ((lane >= V_HEAD - 2) & (lane < V_HEAD))
    is_k = (lane >= K_HEAD - 2) & (lane < K_HEAD + 2)
    edge_taps = [jnp.where(is_k, taps[1][j], taps[2][j]) for j in range(3)]
    far = [jnp.exp(-(rate * float(length * k))) for k in range(n - 1)]
    far_first = jnp.exp(-(rate * (length - 1.0)))
    far_second = jnp.exp(-(rate * (length - 2.0)))
    near_first, near_second = jnp.exp(rate), jnp.exp(2.0 * rate)
    filt_next = jnp.where(lane < 1, 0.0, pltpu.roll(filt, 1, 1))

    for k in range(1, n):
        @pl.when(me >= k)
        def _():
            sends[k - 1].wait_recv()

        @pl.when(me < k)
        def _():
            rcv[k - 1] = jnp.zeros((rows, LANES), jnp.float32)

    def unpack(packed):
        parts = [packed]
        for g in range(1, ch // rows):
            parts.append(pltpu.roll(packed, LANES - g * FIELD, 1))
        return jnp.concatenate(parts, axis=0)

    messages = [unpack(rcv[k - 1]) for k in range(1, n)]
    h0 = jnp.zeros((ch, modes), jnp.float32)
    for k in range(1, n):
        message = messages[k - 1]
        ends = message
        if k + 1 < n:
            ends = jnp.where(
                is_tail, pltpu.roll(messages[k], LANES - (K_TAIL - K_HEAD + 2), 1), message
            )
        shorts = (
            edge_taps[0] * ends
            + edge_taps[1] * pltpu.roll(ends, 1, 1)
            + edge_taps[2] * pltpu.roll(ends, 2, 1)
        ).astype(jnp.bfloat16).astype(jnp.float32)
        firsts = shorts * pltpu.roll(shorts, LANES - (V_HEAD - K_HEAD), 1)
        state = (
            message[:, :modes]
            + far_first * firsts[:, K_HEAD : K_HEAD + 1]
            + far_second * firsts[:, K_HEAD + 1 : K_HEAD + 2]
        )
        h0 = h0 + far[k - 1] * state

    before = messages[0]
    block = pl.ds(0, ch)
    ks = short_block(tile(1, 0), pltpu.roll(before, LANES - 2 - K_TAIL, 1), taps[1], lane)
    vs = short_block(tile(2, 0), pltpu.roll(before, LANES - 2 - V_TAIL, 1), taps[2], lane)
    q_tab[block, :] = short_block(
        tile(0, 0), pltpu.roll(before, LANES - 2 - Q_TAIL, 1), taps[0], lane
    )
    firsts = ks * vs
    one, two = firsts[:, 0:1], firsts[:, 1:2]
    v_tab[block, :] = (
        v_tab[block, :]
        + skip_col * jnp.where(lane < 2, firsts, 0.0)
        + filt * one
        + filt_next * two
    )
    own = near_first * one + near_second * two
    h_in[...] = h0 + own
    h_tab[block, pl.ds(0, modes)] = -own

    def inter(i, carry):
        for j in range(unroll):
            c = i * unroll + j
            hc = h_tab[pl.ds(c, blocks, stride=pit), pl.ds(0, modes)]
            pc = p_tab[pl.ds(c, blocks, stride=pit), pl.ds(0, modes)]
            hc = (hc + pc * h_in[pl.ds(c, 1), :]).astype(jnp.bfloat16)
            gc = g_tab[pl.ds(c, modes, stride=pit), :].astype(jnp.bfloat16)
            z[pl.ds(c, blocks, stride=pit), :] = jnp.dot(
                hc, gc, preferred_element_type=jnp.float32
            )
        return carry

    lax.fori_loop(0, ch // unroll, inter, 0)

    def gate(b, carry):
        at = pl.ds(pl.multiple_of(b * pit, 8), ch)
        value = q_tab[at, :] * (v_tab[at, :] + z[at, :])
        o_ref[:, pl.ds(pl.multiple_of(b * LANES, LANES), LANES)] = value.astype(o_ref.dtype)
        return carry

    lax.fori_loop(0, blocks, gate, 0, unroll=8)

    for k in range(1, n):
        @pl.when(me + k < n)
        def _():
            sends[k - 1].wait_send()


def shards(projections, short_weights, residues, rates, skip):
    n = lax.axis_size("ctx")
    _, ch, length = projections.shape
    modes = residues.shape[1]
    blocks = length // LANES
    pit = ch + PAD
    vmem = pl.BlockSpec(memory_space=pltpu.VMEM)
    hbm = pl.BlockSpec(memory_space=pltpu.HBM)
    return pl.pallas_call(
        functools.partial(kernel, n, 16),
        out_shape=jax.ShapeDtypeStruct((ch, length), jnp.bfloat16),
        in_specs=[hbm] * 5,
        out_specs=vmem,
        scratch_shapes=[
            pltpu.VMEM(short_weights.shape, jnp.float32),
            pltpu.VMEM((modes, ch), jnp.float32),
            pltpu.VMEM((modes, ch), jnp.float32),
            pltpu.VMEM((1, ch), jnp.float32),
            pltpu.VMEM((3, ch, length), jnp.bfloat16),
            pltpu.VMEM((blocks * pit, LANES), jnp.float32),
            pltpu.VMEM((blocks * pit, LANES), jnp.float32),
            pltpu.VMEM((modes * pit, LANES), jnp.float32),
            pltpu.VMEM((modes * pit, LANES), jnp.float32),
            pltpu.VMEM((ch, LANES), jnp.float32),
            pltpu.VMEM((blocks * pit, LANES), jnp.float32),
            pltpu.VMEM((blocks * pit, LANES), jnp.float32),
            pltpu.VMEM((blocks * pit, LANES), jnp.float32),
            pltpu.VMEM((ch, modes), jnp.float32),
            pltpu.VMEM((blocks * pit, LANES), jnp.float32),
            pltpu.VMEM((blocks * pit, LANES), jnp.float32),
            pltpu.VMEM((blocks * pit, LANES), jnp.float32),
            pltpu.VMEM((ch, LANES), jnp.float32),
            pltpu.VMEM((ch * FIELD // LANES, LANES), jnp.float32),
            pltpu.VMEM((n - 1, ch * FIELD // LANES, LANES), jnp.float32),
            pltpu.SemaphoreType.DMA((7,)),
            pltpu.SemaphoreType.DMA((n - 1,)),
            pltpu.SemaphoreType.DMA((n - 1,)),
        ],
        compiler_params=pltpu.CompilerParams(
            collective_id=0, has_side_effects=True, vmem_limit_bytes=32 * 1024 * 1024
        ),
        name="mixer",
    )(*(
        pltpu.with_memory_space_constraint(a, pltpu.HBM)
        for a in (projections, short_weights, residues.T, rates.T, skip[None, :])
    ))


def solution(mesh):
    return jax.shard_map(
        shards,
        mesh=mesh,
        in_specs=(
            P(None, ("groups", "chan"), "ctx"),
            P(None, None, ("groups", "chan")),
            P(("groups", "chan"), None),
            P(("groups", "chan"), None),
            P(("groups", "chan")),
        ),
        out_specs=P(("groups", "chan"), "ctx"),
        check_vma=False,
    )
```
